512 devices in a mesh: rep: 4 (over y), own: 128 (over x, z, core).
Axes of the slice: x: 4, y: 4, z: 16, core: 2. Of those that a mesh axis runs over, the one named last changes fastest.
Arguments:
- local_weights: bfloat16 [4, 192, 384, 768], P('rep', None, 'own'), may hold values from -6 to 6
- anchor: float32 [256, 384, 768], P('own', 'rep'), may hold values from -6 to 6
- momentum: float32 [256, 384, 768], P('own', 'rep'), may hold values from -6 to 6
- owners: int32 [192], replicated, may hold values from 0 to 127, as said below
Outputs:
- new_weights: float32 [192, 384, 768], P(None, 'own')
- new_momentum: float32 [256, 384, 768], P('own', 'rep')
The draws below stay inside these ranges and needn't reach their ends.
Inputs may be any that keep to these rules, and one draw needn't show every extreme that they name: Blocks 2i and 2i+1 for i < 48 form one attention projection and have the same owner; different projections have different owners; the 96 embedding blocks that follow go to the owners holding no projection, in runs of consecutive blocks; every owner holds at least one block and at most 2, and some owner holds exactly 2.
All inputs are finite; a program needn't handle non-finite values.
Results may differ from the reference program's by a relative error of at most 0.0003.
Values may be sent and summed in bfloat16 or wider, within the bound.
A program may use at most 64 MiB of HBM per device.

```python
import jax
import jax.numpy as jnp

D = 768
BLOCK_ROWS = 384
CAP = 2
MATS = 48
BLOCKS = 192
EMB_BLOCKS = 96
N_REP = 4
N_OWN = 128


def draw_owners(key, part):
    first_key, second_key = jax.random.split(jax.random.fold_in(key, 7))
    order = jax.random.permutation(first_key, N_OWN).astype(jnp.int32)
    holders = N_OWN - MATS
    extra = EMB_BLOCKS - holders
    ranks = jax.random.permutation(second_key, holders).astype(jnp.int32)
    counts = (1 + (ranks < extra).astype(jnp.int32)).astype(jnp.int32)
    ends = jnp.cumsum(counts).astype(jnp.int32)
    blocks = jnp.arange(EMB_BLOCKS, dtype=jnp.int32)
    which = jnp.sum((ends[None, :] <= blocks[:, None]).astype(jnp.int32), axis=1).astype(jnp.int32)
    emb_owner = order[MATS + which]
    mat_owner = jnp.repeat(order[:MATS], 2)
    return jnp.concatenate([mat_owner, emb_owner]).astype(jnp.int32)


def level_of(rng, shape, shards, smallest, high):
    def one(axis_at, shards_of):
        heights = jax.random.uniform(jax.random.fold_in(jax.random.fold_in(rng, 6), axis_at), (shards_of,), jnp.float32, smallest / len(shards), high / len(shards))
        return jnp.repeat(jnp.exp(heights), shape[axis_at] // shards_of).reshape((-1,) + (1,) * (len(shape) - axis_at - 1))

    loudness = one(*shards[0])
    for cut in shards[1:]:
        loudness = loudness * one(*cut)
    return loudness


def centred(stream_key, extent, spread, limit, shards=(), held_as=jnp.bfloat16):
    array = jax.random.normal(stream_key, extent, jnp.float32) * spread
    if len(shards) > 0:
        array = level_of(stream_key, extent, shards, -0.22, 0.18) * array
    return jnp.clip(array, min=-limit, max=limit).astype(held_as)


def setup_inputs(seed: int = 0) -> dict:
    arg_keys = jax.random.split(jax.random.key(seed), 5)
    local_weights = centred(arg_keys[0], (N_REP, BLOCKS, BLOCK_ROWS, D), 1.0, 6.0, ((0, 4), (2, 128)))
    anchor = centred(arg_keys[1], (N_OWN * CAP, BLOCK_ROWS, D), 1.0, 6.0, ((0, 128), (1, 4)), jnp.float32)
    momentum = centred(arg_keys[2], (N_OWN * CAP, BLOCK_ROWS, D), 1.0, 6.0, ((0, 128), (1, 4)), jnp.float32)
    owners = draw_owners(jax.random.fold_in(arg_keys[4], 71), 0)
    return dict(local_weights=local_weights, anchor=anchor, momentum=momentum, owners=owners)


outer_rate = 0.7
momentum_rate = 0.9


def reference(local_weights, anchor, momentum, owners):
    index = jnp.arange(BLOCKS, dtype=jnp.int32)
    same = (owners[None, :] == owners[:, None]) & (index[None, :] < index[:, None])
    slot = jnp.sum(same.astype(jnp.int32), axis=1).astype(jnp.int32)
    place = (owners * CAP + slot).astype(jnp.int32)
    mean_local = jnp.sum(local_weights.astype(jnp.float32), axis=0) / N_REP
    held = anchor[place]
    outer_grad = held - mean_local
    moment = momentum_rate * momentum[place] + outer_grad
    new_weights = held - outer_rate * (outer_grad + momentum_rate * moment)
    new_momentum = jnp.zeros(momentum.shape, jnp.float32).at[place].set(moment)
    return new_weights, new_momentum
```

```python
import functools
import math

import jax
import jax.numpy as jnp
from jax import lax
from jax.experimental import pallas as pl
from jax.experimental.pallas import tpu as pltpu
from jax.sharding import PartitionSpec as P

MESH = pl.DeviceIdType.MESH

outer_rate = 0.7
momentum_rate = 0.9
MEAN = outer_rate * (1.0 + momentum_rate)
ANCHOR = 1.0 - MEAN
MOMENT = -outer_rate * momentum_rate * momentum_rate

CURVE = 65536.0
LIMIT = 6.0
BOUND_A = 1.01 * LIMIT * (abs(ANCHOR) + abs(MOMENT))
BOUND_N = 1.01 * LIMIT * (abs(ANCHOR) + abs(MOMENT) + MEAN)
BOUND_D = 1.01 * (LIMIT + BOUND_A / abs(ANCHOR))


def _rate(bound):
    return 32767.0 / math.log(1.0 + CURVE * bound)


def encode(value, bound):
    size = jnp.log(1.0 + CURVE * jnp.abs(value)) * _rate(bound)
    code = (size + 0.5).astype(jnp.int32)
    return jnp.where(value < 0, -code, code)


def decode(code, bound):
    size = jnp.abs(code.astype(jnp.float32))
    value = (jnp.exp(size * (1.0 / _rate(bound))) - 1.0) * (1.0 / CURVE)
    return jnp.where(code < 0, -value, value)


def pack(first, second):
    return (second << 16) | (first & 0xFFFF)


def unpack(pair):
    return (pair << 16) >> 16, pair >> 16


def kernel(
    n_rep, n_p, stripe, width, blocks,
    owners_ref, w_hbm, a_hbm, m_hbm, nw_hbm, nm_hbm,
    w_v, a_v, m_v, nm_v, one_hot, picker, sorted_w, f1_in, a_out, a_in, d_out, d_in, table, out_v,
    load_sem, store_sem, f1_send, f1_recv, a_send, a_recv, d_send, d_recv, n_send, n_recv,
):
    lanes = width // 128
    group = 2 * n_p
    y = lax.axis_index("rep")
    own = lax.axis_index("own")
    x, p = own // n_p, own % n_p
    mine = (2 * x - y + 2 * n_rep) % n_rep
    d_x, d_y = mine, x
    a_x, a_y = y, (2 * y - x + 2 * n_rep) % n_rep
    stays = x == y

    barrier = pltpu.get_barrier_semaphore()

    def greet(i, carry):
        q = (p + i) % n_p

        @pl.when(jnp.logical_not(stays & (i == 0)))
        def _():
            pl.semaphore_signal(barrier, inc=1, device_id=(d_y, d_x * n_p + q), device_id_type=MESH)
            pl.semaphore_signal(barrier, inc=1, device_id=(a_y, a_x * n_p + q), device_id_type=MESH)

        return carry

    lax.fori_loop(0, n_p, greet, 0)
    for step in range(1, n_rep):
        pl.semaphore_signal(barrier, inc=1, device_id=((y + step) % n_rep, own), device_id_type=MESH)

    loads = [pltpu.make_async_copy(w_hbm, w_v, load_sem.at[0])]
    for j in range(lanes):
        columns = pl.ds(128 * j, 128)
        loads.append(pltpu.make_async_copy(a_hbm.at[:, :, columns], a_v.at[j], load_sem.at[1 + j]))
        loads.append(pltpu.make_async_copy(m_hbm.at[:, :, columns], m_v.at[j], load_sem.at[1 + lanes + j]))
    for load in loads:
        load.start()

    row = jnp.broadcast_to(owners_ref[...], (blocks, blocks)).astype(jnp.float32)
    first = lax.broadcasted_iota(jnp.int32, (blocks, blocks), 0)
    second = lax.broadcasted_iota(jnp.int32, (blocks, blocks), 1)
    column = jnp.sum(jnp.where(first == second, row, 0.0), axis=1, keepdims=True)
    same = jnp.where(row == column, 1.0, 0.0)
    slot_row = jnp.sum(jnp.where(first < second, same, 0.0), axis=0, keepdims=True)
    slot_column = jnp.sum(jnp.where(second < first, same, 0.0), axis=1, keepdims=True)
    place_row = 2.0 * row[:1] + slot_row
    place_column = 2.0 * column + slot_column
    slots = n_rep * group
    j = lax.broadcasted_iota(jnp.int32, (slots, blocks), 0)
    target = 2 * (j // group * n_p + j % n_p) + j % group // n_p
    one_hot[...] = jnp.where(place_row == target.astype(jnp.float32), 1.0, 0.0).astype(jnp.bfloat16)
    j = lax.broadcasted_iota(jnp.int32, (blocks, slots), 1)
    target = 2 * (j % (n_rep * n_p)) + j // (n_rep * n_p)
    picker[...] = jnp.where(place_column == target.astype(jnp.float32), 1.0, 0.0).astype(jnp.bfloat16)
    alive = []
    for s in range(2):
        here = (2 * own + s).astype(jnp.float32)
        alive.append(jnp.max(jnp.where(place_row == here, 1.0, 0.0), axis=1, keepdims=True) > 0.5)

    for load in loads[1:]:
        load.wait()
    for k in range(stripe):
        for j in range(lanes):
            codes = []
            for s in range(2):
                rows = (j, s, pl.ds(k, n_p, stride=stripe), slice(None))
                codes.append(encode(ANCHOR * a_v[rows] + MOMENT * m_v[rows], BOUND_A))
            a_out[:, pl.ds(k * width + 128 * j, 128)] = pack(*codes)

    loads[0].wait()
    for k in range(stripe):
        moved = jnp.dot(one_hot[...], w_v[k], preferred_element_type=jnp.float32)
        sorted_w[:, k] = moved.astype(jnp.bfloat16).reshape(n_rep, group, width)

    pl.semaphore_wait(barrier, n_rep - 1 + 2 * jnp.where(stays, n_p - 1, n_p))

    def to_rep(source, target_of, send, recv, step, tag):
        return pltpu.make_async_remote_copy(
            src_ref=source, dst_ref=target_of, send_sem=send.at[step - 1], recv_sem=recv.at[tag],
            device_id=((y + step) % n_rep, own), device_id_type=MESH,
        )

    f1 = []
    for step in range(1, n_rep):
        theirs = (2 * x - (y + step) + 2 * n_rep) % n_rep
        f1.append(to_rep(sorted_w.at[theirs], f1_in.at[step - 1], f1_send, f1_recv, step, step - 1))
        f1[-1].start()

    def row_copy(source, target, send, recv, to_y, to_x, q):
        return pltpu.make_async_remote_copy(
            src_ref=source.at[pl.ds(q, 1)], dst_ref=target.at[pl.ds(p, 1)], send_sem=send.at[q], recv_sem=recv.at[p],
            device_id=(to_y, to_x * n_p + q), device_id_type=MESH,
        )

    def own_row(source, target, recv):
        return pltpu.make_async_copy(source.at[pl.ds(p, 1)], target.at[pl.ds(p, 1)], recv.at[p])

    def spread(source, target, send, recv, to_y, to_x):
        def one(i, carry):
            q = (p + i) % n_p
            local = stays & (i == 0)

            @pl.when(local)
            def _():
                own_row(source, target, recv).start()

            @pl.when(jnp.logical_not(local))
            def _():
                row_copy(source, target, send, recv, to_y, to_x, q).start()

            return carry

        lax.fori_loop(0, n_p, one, 0)

    def collect(target, recv):
        def one(q, carry):
            pltpu.make_async_copy(target.at[pl.ds(q, 1)], target.at[pl.ds(q, 1)], recv.at[q]).wait()
            return carry

        lax.fori_loop(0, n_p, one, 0)

    def settle(source, target, send, recv, to_y, to_x):
        def one(i, carry):
            q = (p + i) % n_p

            @pl.when(jnp.logical_not(stays & (i == 0)))
            def _():
                row_copy(source, target, send, recv, to_y, to_x, q).wait_send()

            return carry

        lax.fori_loop(0, n_p, one, 0)

    spread(a_out, a_in, a_send, a_recv, a_y, a_x)

    for copy in f1:
        copy.wait_recv()
    collect(a_in, a_recv)
    for k in range(stripe):
        for j in range(0, width, 256):
            columns = pl.ds(j, 256)
            total = sorted_w[mine, k, :, columns].astype(jnp.float32)
            for step in range(1, n_rep):
                total += f1_in[step - 1, k, :, columns].astype(jnp.float32)
            mean = total * (1.0 / n_rep)
            shares = unpack(a_in[:, pl.ds(k * width + j, 256)])
            new_codes, mean_codes = [], []
            for s in range(2):
                share = decode(shares[s], BOUND_A)
                here = mean[s * n_p : (s + 1) * n_p]
                new_codes.append(encode(share + MEAN * here, BOUND_N))
                mean_codes.append(encode(here - (1.0 / ANCHOR) * share, BOUND_D))
            table[mine, k, :, columns] = pack(*new_codes)
            d_out[:, pl.ds(k * width + j, 256)] = pack(*mean_codes)

    spread(d_out, d_in, d_send, d_recv, d_y, d_x)
    gather = []
    for step in range(1, n_rep):
        gather.append(to_rep(table.at[mine], table.at[mine], n_send, n_recv, step, step - 1))
        gather[-1].start()

    collect(d_in, d_recv)
    for k in range(stripe):
        for j in range(lanes):
            columns = pl.ds(k * width + 128 * j, 128)
            shares, gaps = unpack(a_out[:, columns]), unpack(d_in[:, columns])
            for s in range(2):
                rows = (j, s, pl.ds(k, n_p, stride=stripe), slice(None))
                mean = decode(gaps[s], BOUND_D) + (1.0 / ANCHOR) * decode(shares[s], BOUND_A)
                moment = momentum_rate * m_v[rows] + (a_v[rows] - mean)
                nm_v[rows] = jnp.where(alive[s], moment, 0.0)
    stores = []
    for j in range(lanes):
        stores.append(pltpu.make_async_copy(nm_v.at[j], nm_hbm.at[:, :, pl.ds(128 * j, 128)], store_sem.at[j]))
        stores[-1].start()

    for copy in gather:
        copy.wait_recv()
    for k in range(stripe):
        pairs = table[:, k].reshape(n_rep * n_p, width)
        low = jnp.concatenate([pairs & 255, (pairs >> 16) & 255], axis=0)
        high = jnp.concatenate([(pairs >> 8) & 255, pairs >> 24], axis=0)
        picked = []
        for part in (low, high):
            part = part.astype(jnp.float32).astype(jnp.bfloat16)
            picked.append(jnp.dot(picker[...], part, preferred_element_type=jnp.float32))
        code = picked[0] + 256.0 * picked[1]
        code = jnp.where(code >= 32768.0, code - 65536.0, code)
        out_v[k] = decode(code, BOUND_N)
        stores.append(pltpu.make_async_copy(out_v.at[k], nw_hbm.at[k], store_sem.at[lanes + k]))
        stores[-1].start()

    for copy in f1 + gather:
        copy.wait_send()
    settle(a_out, a_in, a_send, a_recv, a_y, a_x)
    settle(d_out, d_in, d_send, d_recv, d_y, d_x)
    for store in stores:
        store.wait()


def local(local_weights, anchor, momentum, owners):
    n_rep = lax.axis_size("rep")
    n_p = lax.axis_size("own") // n_rep
    blocks = owners.shape[0]
    stripe, width = local_weights.shape[2:]
    lanes = width // 128
    group = 2 * n_p
    rows = jnp.transpose(local_weights[0], (1, 0, 2))
    tall = (lanes, *anchor.shape[:2], 128)
    pairs = (n_p, stripe * width)
    vmem, dma = pltpu.VMEM, pltpu.SemaphoreType.DMA
    new_weights, new_momentum = pl.pallas_call(
        functools.partial(kernel, n_rep, n_p, stripe, width, blocks),
        out_shape=(
            jax.ShapeDtypeStruct(rows.shape, jnp.float32),
            jax.ShapeDtypeStruct(momentum.shape, jnp.float32),
        ),
        in_specs=[pl.BlockSpec(memory_space=pltpu.VMEM)] + [pl.BlockSpec(memory_space=pl.ANY)] * 3,
        out_specs=(pl.BlockSpec(memory_space=pl.ANY),) * 2,
        scratch_shapes=[
            vmem(rows.shape, jnp.bfloat16),
            vmem(tall, jnp.float32),
            vmem(tall, jnp.float32),
            vmem(tall, jnp.float32),
            vmem((n_rep * group, blocks), jnp.bfloat16),
            vmem((blocks, n_rep * group), jnp.bfloat16),
            vmem((n_rep, stripe, group, width), jnp.bfloat16),
            vmem((n_rep - 1, stripe, group, width), jnp.bfloat16),
            vmem(pairs, jnp.int32),
            vmem(pairs, jnp.int32),
            vmem(pairs, jnp.int32),
            vmem(pairs, jnp.int32),
            vmem((n_rep, stripe, n_p, width), jnp.int32),
            vmem(rows.shape, jnp.float32),
            dma((1 + 2 * lanes,)),
            dma((lanes + stripe,)),
            dma((n_rep - 1,)),
            dma((n_rep - 1,)),
            dma((n_p,)),
            dma((n_p,)),
            dma((n_p,)),
            dma((n_p,)),
            dma((n_rep - 1,)),
            dma((n_rep - 1,)),
        ],
        compiler_params=pltpu.CompilerParams(collective_id=0, has_side_effects=True, vmem_limit_bytes=48 << 20),
    )(owners.reshape(1, blocks), rows, anchor, momentum)
    return jnp.transpose(new_weights, (1, 0, 2)), new_momentum


def solution(mesh):
    return jax.shard_map(
        local,
        mesh=mesh,
        in_specs=(P("rep", None, "own", None), P("own", "rep", None), P("own", "rep", None), P()),
        out_specs=(P(None, "own", None), P("own", "rep", None)),
        check_vma=False,
    )
```

```python
import functools
import math

import jax
import jax.numpy as jnp
from jax import lax
from jax.experimental import pallas as pl
from jax.experimental.pallas import tpu as pltpu
from jax.sharding import PartitionSpec as P

MESH = pl.DeviceIdType.MESH

outer_rate = 0.7
momentum_rate = 0.9
MEAN = outer_rate * (1.0 + momentum_rate)
ANCHOR = 1.0 - MEAN
MOMENT = -outer_rate * momentum_rate * momentum_rate

CURVE = 65536.0
LIMIT = 6.0
BOUND_A = 1.01 * LIMIT * (abs(ANCHOR) + abs(MOMENT))
BOUND_N = 1.01 * LIMIT * (abs(ANCHOR) + abs(MOMENT) + MEAN)
BOUND_D = 1.01 * (LIMIT + BOUND_A / abs(ANCHOR))


def _rate(bound):
    return 32767.0 / math.log(1.0 + CURVE * bound)


def encode(value, bound):
    size = jnp.log(1.0 + CURVE * jnp.abs(value)) * _rate(bound)
    code = (size + 0.5).astype(jnp.int32)
    return jnp.where(value < 0, -code, code)


def decode(code, bound):
    size = jnp.abs(code.astype(jnp.float32))
    value = (jnp.exp(size * (1.0 / _rate(bound))) - 1.0) * (1.0 / CURVE)
    return jnp.where(code < 0, -value, value)


def pack(first, second):
    return (second << 16) | (first & 0xFFFF)


def unpack(pair):
    return (pair << 16) >> 16, pair >> 16


def kernel(
    n_rep, n_p, stripe, width, blocks,
    owners_hbm, w_hbm, a_hbm, m_hbm, nw_hbm, nm_hbm,
    owners_v, w_v, a_v, m_v, nm_v, one_hot, picker, sorted_w, f1_in, a_out, a_in, d_out, d_in, table, out_v,
    load_sem, store_sem, f1_send, f1_recv, a_send, a_recv, d_send, d_recv, r_send, r_recv, t_send, t_recv,
):
    lanes = width // 128
    group = 2 * n_p
    y = lax.axis_index("rep")
    own = lax.axis_index("own")
    x, p = own // n_p, own % n_p
    diagonal = x == y

    barrier = pltpu.get_barrier_semaphore()

    def hello(to_y, to_own):
        pl.semaphore_signal(barrier, inc=1, device_id=(to_y, to_own), device_id_type=MESH)

    def greet(i, carry):
        hello(y, x * n_p + (p + i) % n_p)
        return carry

    lax.fori_loop(1, n_p, greet, 0)
    for i in range(1, n_rep):
        hello((y + i) % n_rep, own)
        hello(y, (x + i) % n_rep * n_p + p)
    for i in range(n_rep):

        @pl.when(jnp.logical_not(diagonal & (x == i)))
        def _():
            hello(x, i * n_p + p)
            hello(i, y * n_p + p)

    loads = [pltpu.make_async_copy(owners_hbm, owners_v, load_sem.at[0])]
    for j in range(lanes):
        columns = pl.ds(128 * j, 128)
        loads.append(pltpu.make_async_copy(a_hbm.at[:, :, columns], a_v.at[j], load_sem.at[2 + j]))
        loads.append(pltpu.make_async_copy(m_hbm.at[:, :, columns], m_v.at[j], load_sem.at[2 + lanes + j]))
    loads.append(pltpu.make_async_copy(w_hbm, w_v, load_sem.at[1]))
    for load in loads:
        load.start()

    loads[0].wait()
    row = jnp.broadcast_to(owners_v[...], (blocks, blocks)).astype(jnp.float32)
    first = lax.broadcasted_iota(jnp.int32, (blocks, blocks), 0)
    second = lax.broadcasted_iota(jnp.int32, (blocks, blocks), 1)
    column = jnp.sum(jnp.where(first == second, row, 0.0), axis=1, keepdims=True)
    same = jnp.where(row == column, 1.0, 0.0)
    slot_row = jnp.sum(jnp.where(first < second, same, 0.0), axis=0, keepdims=True)
    slot_column = jnp.sum(jnp.where(second < first, same, 0.0), axis=1, keepdims=True)
    place_row = 2.0 * row[:1] + slot_row
    place_column = 2.0 * column + slot_column
    slots = n_rep * group
    j = lax.broadcasted_iota(jnp.int32, (slots, blocks), 0)
    target = 2 * (j // group * n_p + j % n_p) + j % group // n_p
    one_hot[...] = jnp.where(place_row == target.astype(jnp.float32), 1.0, 0.0).astype(jnp.bfloat16)
    j = lax.broadcasted_iota(jnp.int32, (blocks, slots), 1)
    target = 2 * (j % (n_rep * n_p)) + j // (n_rep * n_p)
    picker[...] = jnp.where(place_column == target.astype(jnp.float32), 1.0, 0.0).astype(jnp.bfloat16)
    alive = []
    for s in range(2):
        here = (2 * own + s).astype(jnp.float32)
        alive.append(jnp.max(jnp.where(place_row == here, 1.0, 0.0), axis=1, keepdims=True) > 0.5)

    for load in loads[1:]:
        load.wait()
    for k in range(stripe):
        for j in range(lanes):
            codes = []
            for s in range(2):
                rows = (j, s, pl.ds(k, n_p, stride=stripe), slice(None))
                codes.append(encode(ANCHOR * a_v[rows] + MOMENT * m_v[rows], BOUND_A))
            a_out[k, :, pl.ds(128 * j, 128)] = pack(*codes)

    for k in range(stripe):
        moved = jnp.dot(one_hot[...], w_v[k], preferred_element_type=jnp.float32)
        sorted_w[:, k] = moved.astype(jnp.bfloat16).reshape(n_rep, group, width)

    pl.semaphore_wait(barrier, n_p - 1 + 2 * (n_rep - 1) + 2 * jnp.where(diagonal, n_rep - 1, n_rep))

    def row_copy(source, target, send, recv, k, q):
        return pltpu.make_async_remote_copy(
            src_ref=source.at[k, pl.ds(q, 1)], dst_ref=target.at[k, pl.ds(p, 1)],
            send_sem=send.at[k, q], recv_sem=recv.at[k, p], device_id=(y, x * n_p + q), device_id_type=MESH,
        )

    def spread(source, target, send, recv, k):
        rows = pl.ds(p, 1)
        pltpu.make_async_copy(source.at[k, rows], target.at[k, rows], recv.at[k, p]).start()

        def one(i, carry):
            row_copy(source, target, send, recv, k, (p + i) % n_p).start()
            return carry

        lax.fori_loop(1, n_p, one, 0)

    def collect(target, recv, k):
        def one(q, carry):
            rows = target.at[k, pl.ds(q, 1)]
            pltpu.make_async_copy(rows, rows, recv.at[k, q]).wait()
            return carry

        lax.fori_loop(0, n_p, one, 0)

    def settle(source, target, send, recv, k):
        def one(i, carry):
            row_copy(source, target, send, recv, k, (p + i) % n_p).wait_send()
            return carry

        lax.fori_loop(1, n_p, one, 0)

    def f1_copy(k, g):
        return pltpu.make_async_remote_copy(
            src_ref=sorted_w.at[g, k], dst_ref=f1_in.at[y, k], send_sem=f1_send.at[k, g], recv_sem=f1_recv.at[k, y],
            device_id=(x, g * n_p + p), device_id_type=MESH,
        )

    for k in range(stripe):
        for i in range(n_rep):
            g = (x + 1 + i) % n_rep
            stays = diagonal & (g == x)

            @pl.when(stays)
            def _():
                pltpu.make_async_copy(sorted_w.at[g, k], f1_in.at[y, k], f1_recv.at[k, y]).start()

            @pl.when(jnp.logical_not(stays))
            def _():
                f1_copy(k, g).start()

        spread(a_out, a_in, a_send, a_recv, k)

    def spot(plane):
        return jnp.where(plane == x, x, n_rep + plane)

    def pass_on(k, plane):
        return pltpu.make_async_remote_copy(
            src_ref=table.at[n_rep + plane, k], dst_ref=table.at[x, k], send_sem=t_send.at[k, plane],
            recv_sem=t_recv.at[k, x], device_id=(y, plane * n_p + p), device_id_type=MESH,
        )

    def start_pass_on(k, plane):
        @pl.when(plane != x)
        def _():
            pass_on(k, plane).start()

    def r_copy(k, step):
        return pltpu.make_async_remote_copy(
            src_ref=table.at[spot(y), k], dst_ref=table.at[spot(y), k], send_sem=r_send.at[k, step - 1],
            recv_sem=r_recv.at[k, y], device_id=((y + step) % n_rep, own), device_id_type=MESH,
        )

    def relay(k):
        for step in sorted(range(1, n_rep), key=lambda step: min(step, n_rep - step)):
            plane = (y + step) % n_rep
            place = table.at[spot(plane), k]
            pltpu.make_async_copy(place, place, r_recv.at[k, plane]).wait()
            start_pass_on(k, plane)

    for k in range(stripe):
        for i in range(n_rep):
            pltpu.make_async_copy(f1_in.at[i, k], f1_in.at[i, k], f1_recv.at[k, i]).wait()
        collect(a_in, a_recv, k)
        for j in range(0, width, 256):
            columns = pl.ds(j, 256)
            total = f1_in[0, k, :, columns].astype(jnp.float32)
            for i in range(1, n_rep):
                total += f1_in[i, k, :, columns].astype(jnp.float32)
            mean = total * (1.0 / n_rep)
            shares = unpack(a_in[k, :, columns])
            new_codes, mean_codes = [], []
            for s in range(2):
                share = decode(shares[s], BOUND_A)
                here = mean[s * n_p : (s + 1) * n_p]
                new_codes.append(encode(share + MEAN * here, BOUND_N))
                mean_codes.append(encode(here - (1.0 / ANCHOR) * share, BOUND_D))
            table[spot(y), k, :, columns] = pack(*new_codes)
            d_out[k, :, columns] = pack(*mean_codes)
        for step in sorted(range(1, n_rep), key=lambda step: -min(step, n_rep - step)):
            r_copy(k, step).start()
        start_pass_on(k, y)
        spread(d_out, d_in, d_send, d_recv, k)
        if k > 0:
            relay(k - 1)
    relay(stripe - 1)

    for k in range(stripe):
        collect(d_in, d_recv, k)
        for j in range(lanes):
            columns = pl.ds(128 * j, 128)
            shares, gaps = unpack(a_out[k, :, columns]), unpack(d_in[k, :, columns])
            for s in range(2):
                rows = (j, s, pl.ds(k, n_p, stride=stripe), slice(None))
                mean = decode(gaps[s], BOUND_D) + (1.0 / ANCHOR) * decode(shares[s], BOUND_A)
                moment = momentum_rate * m_v[rows] + (a_v[rows] - mean)
                nm_v[rows] = jnp.where(alive[s], moment, 0.0)
    stores = []
    for j in range(lanes):
        stores.append(pltpu.make_async_copy(nm_v.at[j], nm_hbm.at[:, :, pl.ds(128 * j, 128)], store_sem.at[j]))
        stores[-1].start()

    for k in range(stripe):
        for i in range(1, n_rep):
            there = (x + i) % n_rep
            place = table.at[there, k]
            pltpu.make_async_copy(place, place, t_recv.at[k, there]).wait()
        pairs = table[:n_rep, k].reshape(n_rep * n_p, width)
        low = jnp.concatenate([pairs & 255, (pairs >> 16) & 255], axis=0)
        high = jnp.concatenate([(pairs >> 8) & 255, pairs >> 24], axis=0)
        picked = []
        for part in (low, high):
            part = part.astype(jnp.float32).astype(jnp.bfloat16)
            picked.append(jnp.dot(picker[...], part, preferred_element_type=jnp.float32))
        code = picked[0] + 256.0 * picked[1]
        code = jnp.where(code >= 32768.0, code - 65536.0, code)
        out_v[k] = decode(code, BOUND_N)
        stores.append(pltpu.make_async_copy(out_v.at[k], nw_hbm.at[k], store_sem.at[lanes + k]))
        stores[-1].start()

    for k in range(stripe):
        for i in range(n_rep):

            @pl.when(jnp.logical_not(diagonal & (x == i)))
            def _():
                f1_copy(k, i).wait_send()

            @pl.when(x != i)
            def _():
                pass_on(k, i).wait_send()

        for step in range(1, n_rep):
            r_copy(k, step).wait_send()
        settle(a_out, a_in, a_send, a_recv, k)
        settle(d_out, d_in, d_send, d_recv, k)
    for store in stores:
        store.wait()


def local(local_weights, anchor, momentum, owners):
    n_rep = lax.axis_size("rep")
    n_p = lax.axis_size("own") // n_rep
    blocks = owners.shape[0]
    stripe, width = local_weights.shape[2:]
    lanes = width // 128
    group = 2 * n_p
    rows = jnp.transpose(local_weights[0], (1, 0, 2))
    tall = (lanes, *anchor.shape[:2], 128)
    pairs = (stripe, n_p, width)
    vmem, dma = pltpu.VMEM, pltpu.SemaphoreType.DMA
    new_weights, new_momentum = pl.pallas_call(
        functools.partial(kernel, n_rep, n_p, stripe, width, blocks),
        out_shape=(
            jax.ShapeDtypeStruct(rows.shape, jnp.float32),
            jax.ShapeDtypeStruct(momentum.shape, jnp.float32),
        ),
        in_specs=[pl.BlockSpec(memory_space=pl.ANY)] * 4,
        out_specs=(pl.BlockSpec(memory_space=pl.ANY),) * 2,
        scratch_shapes=[
            vmem((1, blocks), jnp.int32),
            vmem(rows.shape, jnp.bfloat16),
            vmem(tall, jnp.float32),
            vmem(tall, jnp.float32),
            vmem(tall, jnp.float32),
            vmem((n_rep * group, blocks), jnp.bfloat16),
            vmem((blocks, n_rep * group), jnp.bfloat16),
            vmem((n_rep, stripe, group, width), jnp.bfloat16),
            vmem((n_rep, stripe, group, width), jnp.bfloat16),
            vmem(pairs, jnp.int32),
            vmem(pairs, jnp.int32),
            vmem(pairs, jnp.int32),
            vmem(pairs, jnp.int32),
            vmem((2 * n_rep, *pairs), jnp.int32),
            vmem(rows.shape, jnp.float32),
            dma((2 + 2 * lanes,)),
            dma((lanes + stripe,)),
            dma((stripe, n_rep)),
            dma((stripe, n_rep)),
            dma((stripe, n_p)),
            dma((stripe, n_p)),
            dma((stripe, n_p)),
            dma((stripe, n_p)),
            dma((stripe, n_rep - 1)),
            dma((stripe, n_rep)),
            dma((stripe, n_rep)),
            dma((stripe, n_rep)),
        ],
        compiler_params=pltpu.CompilerParams(collective_id=0, has_side_effects=True, vmem_limit_bytes=64000000),
    )(owners.reshape(1, blocks), rows, anchor, momentum)
    return jnp.transpose(new_weights, (1, 0, 2)), new_momentum


def solution(mesh):
    return jax.shard_map(
        local,
        mesh=mesh,
        in_specs=(P("rep", None, "own", None), P("own", "rep", None), P("own", "rep", None), P()),
        out_specs=(P(None, "own", None), P("own", "rep", None)),
        check_vma=False,
    )
```

```python
import functools
import math

import jax
import jax.numpy as jnp
from jax import lax
from jax.experimental import pallas as pl
from jax.experimental.pallas import tpu as pltpu
from jax.sharding import PartitionSpec as P

MESH = pl.DeviceIdType.MESH

outer_rate = 0.7
momentum_rate = 0.9
MEAN = outer_rate * (1.0 + momentum_rate)
ANCHOR = 1.0 - MEAN
MOMENT = -outer_rate * momentum_rate * momentum_rate

CURVE = 65536.0
LIMIT = 6.0
BOUND_A = 1.01 * LIMIT * (abs(ANCHOR) + abs(MOMENT))
BOUND_N = 1.01 * LIMIT * (abs(ANCHOR) + abs(MOMENT) + MEAN)
BOUND_D = 1.01 * (LIMIT + BOUND_A / abs(ANCHOR))


def _rate(bound):
    return 32767.0 / math.log(1.0 + CURVE * bound)


def encode(value, bound):
    size = jnp.log(1.0 + CURVE * jnp.abs(value)) * _rate(bound)
    code = (size + 0.5).astype(jnp.int32)
    return jnp.where(value < 0, -code, code)


def decode(code, bound):
    size = jnp.abs(code.astype(jnp.float32))
    value = (jnp.exp(size * (1.0 / _rate(bound))) - 1.0) * (1.0 / CURVE)
    return jnp.where(code < 0, -value, value)


def pack(first, second):
    return (second << 16) | (first & 0xFFFF)


def unpack(pair):
    return (pair << 16) >> 16, pair >> 16


def kernel(
    n_rep, n_p, stripe, width, blocks,
    owners_hbm, w_hbm, a_hbm, m_hbm, nw_hbm, nm_hbm,
    owners_v, w_v, a_v, m_v, nm_v, one_hot, picker, sorted_w, f1_in, a_out, a_in, d_out, d_in, table, out_v,
    load_sem, store_sem, f1_send, f1_recv, a_send, a_recv, d_send, d_recv, r_send, r_recv, t_send, t_recv, far_sem, near_sem,
):
    lanes = width // 128
    group = 2 * n_p
    y = lax.axis_index("rep")
    own = lax.axis_index("own")
    x, p = own // n_p, own % n_p
    diagonal = x == y

    barrier = pltpu.get_barrier_semaphore()

    def hello(to_y, to_own):
        pl.semaphore_signal(barrier, inc=1, device_id=(to_y, to_own), device_id_type=MESH)

    n_z = n_p // 2
    half = (n_z // 2 + 1) // 2
    z, core = p // 2, p % 2
    reach = [step for step in range(1, n_z) if min(step, n_z - step) <= half]
    jumps = sorted({half, n_z - half})
    partner = x * n_p + 2 * z + 1 - core

    def ring(step):
        return x * n_p + 2 * ((z + step) % n_z) + core

    for step in reach:
        hello(y, ring(step))
    hello(y, partner)
    for i in range(1, n_rep):
        hello((y + i) % n_rep, own)
        hello(y, (x + i) % n_rep * n_p + p)
    for i in range(n_rep):

        @pl.when(jnp.logical_not(diagonal & (x == i)))
        def _():
            hello(x, i * n_p + p)
            hello(i, y * n_p + p)

    loads = [pltpu.make_async_copy(owners_hbm, owners_v, load_sem.at[0])]
    for j in range(lanes):
        columns = pl.ds(128 * j, 128)
        loads.append(pltpu.make_async_copy(a_hbm.at[:, :, columns], a_v.at[j], load_sem.at[2 + j]))
        loads.append(pltpu.make_async_copy(m_hbm.at[:, :, columns], m_v.at[j], load_sem.at[2 + lanes + j]))
    loads.append(pltpu.make_async_copy(w_hbm, w_v, load_sem.at[1]))
    for load in loads:
        load.start()

    loads[0].wait()
    row = jnp.broadcast_to(owners_v[...], (blocks, blocks)).astype(jnp.float32)
    first = lax.broadcasted_iota(jnp.int32, (blocks, blocks), 0)
    second = lax.broadcasted_iota(jnp.int32, (blocks, blocks), 1)
    column = jnp.sum(jnp.where(first == second, row, 0.0), axis=1, keepdims=True)
    same = jnp.where(row == column, 1.0, 0.0)
    slot_row = jnp.sum(jnp.where(first < second, same, 0.0), axis=0, keepdims=True)
    slot_column = jnp.sum(jnp.where(second < first, same, 0.0), axis=1, keepdims=True)
    place_row = 2.0 * row[:1] + slot_row
    place_column = 2.0 * column + slot_column
    slots = n_rep * group
    j = lax.broadcasted_iota(jnp.int32, (slots, blocks), 0)
    target = 2 * (j // group * n_p + j % n_p) + j % group // n_p
    one_hot[...] = jnp.where(place_row == target.astype(jnp.float32), 1.0, 0.0).astype(jnp.bfloat16)
    j = lax.broadcasted_iota(jnp.int32, (blocks, slots), 1)
    target = 2 * (j % (n_rep * n_p)) + j // (n_rep * n_p)
    picker[...] = jnp.where(place_column == target.astype(jnp.float32), 1.0, 0.0).astype(jnp.bfloat16)
    alive = []
    for s in range(2):
        here = (2 * own + s).astype(jnp.float32)
        alive.append(jnp.max(jnp.where(place_row == here, 1.0, 0.0), axis=1, keepdims=True) > 0.5)

    loads[-1].wait()
    for k in range(stripe):
        moved = jnp.dot(one_hot[...], w_v[k], preferred_element_type=jnp.float32)
        sorted_w[:, k] = moved.astype(jnp.bfloat16).reshape(n_rep, group, width)

    pl.semaphore_wait(barrier, len(reach) + 1 + 2 * (n_rep - 1) + 2 * jnp.where(diagonal, n_rep - 1, n_rep))
    for i, step in enumerate(jumps):
        pl.semaphore_signal(far_sem.at[i], inc=1, device_id=(y, ring(step)), device_id_type=MESH)

    def row_copy(source, target, send, recv, k, q):
        return pltpu.make_async_remote_copy(
            src_ref=source.at[k, pl.ds(q, 1)], dst_ref=target.at[k, pl.ds(p, 1)],
            send_sem=send.at[k, q], recv_sem=recv.at[k, p], device_id=(y, x * n_p + q), device_id_type=MESH,
        )

    def spread(source, target, send, recv, k):
        rows = pl.ds(p, 1)
        pltpu.make_async_copy(source.at[k, rows], target.at[k, rows], recv.at[k, p]).start()

        def one(i, carry):
            row_copy(source, target, send, recv, k, (p + i) % n_p).start()
            return carry

        lax.fori_loop(1, n_p, one, 0)

    def collect(target, recv, k):
        def one(q, carry):
            rows = target.at[k, pl.ds(q, 1)]
            pltpu.make_async_copy(rows, rows, recv.at[k, q]).wait()
            return carry

        lax.fori_loop(0, n_p, one, 0)

    def settle(source, target, send, recv, k):
        def one(i, carry):
            row_copy(source, target, send, recv, k, (p + i) % n_p).wait_send()
            return carry

        lax.fori_loop(1, n_p, one, 0)

    def f1_copy(k, g):
        return pltpu.make_async_remote_copy(
            src_ref=sorted_w.at[g, k], dst_ref=f1_in.at[y, k], send_sem=f1_send.at[k, g], recv_sem=f1_recv.at[k, y],
            device_id=(x, g * n_p + p), device_id_type=MESH,
        )

    for k in range(stripe):
        for i in range(n_rep):
            g = (x + 1 + i) % n_rep
            stays = diagonal & (g == x)

            @pl.when(stays)
            def _():
                pltpu.make_async_copy(sorted_w.at[g, k], f1_in.at[y, k], f1_recv.at[k, y]).start()

            @pl.when(jnp.logical_not(stays))
            def _():
                f1_copy(k, g).start()

    for load in loads[1:-1]:
        load.wait()
    for k in range(stripe):
        for j in range(lanes):
            codes = []
            for s in range(2):
                rows = (j, s, pl.ds(k, n_p, stride=stripe), slice(None))
                codes.append(encode(ANCHOR * a_v[rows] + MOMENT * m_v[rows], BOUND_A))
            a_out[k, :, pl.ds(128 * j, 128)] = pack(*codes)

    for i in range(len(jumps)):
        pl.semaphore_wait(far_sem.at[i], 1)
    pl.semaphore_signal(near_sem, inc=1, device_id=(y, partner), device_id_type=MESH)
    pl.semaphore_wait(near_sem, 1)
    for k in range(stripe):
        spread(a_out, a_in, a_send, a_recv, k)

    def spot(plane):
        return jnp.where(plane == x, x, n_rep + plane)

    def pass_on(k, plane):
        return pltpu.make_async_remote_copy(
            src_ref=table.at[n_rep + plane, k], dst_ref=table.at[x, k], send_sem=t_send.at[k, plane],
            recv_sem=t_recv.at[k, x], device_id=(y, plane * n_p + p), device_id_type=MESH,
        )

    def start_pass_on(k, plane):
        @pl.when(plane != x)
        def _():
            pass_on(k, plane).start()

    def r_copy(k, step):
        return pltpu.make_async_remote_copy(
            src_ref=table.at[spot(y), k], dst_ref=table.at[spot(y), k], send_sem=r_send.at[k, step - 1],
            recv_sem=r_recv.at[k, y], device_id=((y + step) % n_rep, own), device_id_type=MESH,
        )

    def relay(k):
        for step in sorted(range(1, n_rep), key=lambda step: min(step, n_rep - step)):
            plane = (y + step) % n_rep
            place = table.at[spot(plane), k]
            pltpu.make_async_copy(place, place, r_recv.at[k, plane]).wait()
            start_pass_on(k, plane)

    for k in range(stripe):
        for i in range(n_rep):
            pltpu.make_async_copy(f1_in.at[i, k], f1_in.at[i, k], f1_recv.at[k, i]).wait()
        collect(a_in, a_recv, k)
        for j in range(0, width, 256):
            columns = pl.ds(j, 256)
            total = f1_in[0, k, :, columns].astype(jnp.float32)
            for i in range(1, n_rep):
                total += f1_in[i, k, :, columns].astype(jnp.float32)
            mean = total * (1.0 / n_rep)
            shares = unpack(a_in[k, :, columns])
            new_codes, mean_codes = [], []
            for s in range(2):
                share = decode(shares[s], BOUND_A)
                here = mean[s * n_p : (s + 1) * n_p]
                new_codes.append(encode(share + MEAN * here, BOUND_N))
                mean_codes.append(encode(here - (1.0 / ANCHOR) * share, BOUND_D))
            table[spot(y), k, :, columns] = pack(*new_codes)
            d_out[k, :, columns] = pack(*mean_codes)
        for step in sorted(range(1, n_rep), key=lambda step: -min(step, n_rep - step)):
            r_copy(k, step).start()
        start_pass_on(k, y)
        spread(d_out, d_in, d_send, d_recv, k)
        if k > 0:
            relay(k - 1)
    relay(stripe - 1)

    for k in range(stripe):
        collect(d_in, d_recv, k)
        for j in range(lanes):
            columns = pl.ds(128 * j, 128)
            shares, gaps = unpack(a_out[k, :, columns]), unpack(d_in[k, :, columns])
            for s in range(2):
                rows = (j, s, pl.ds(k, n_p, stride=stripe), slice(None))
                mean = decode(gaps[s], BOUND_D) + (1.0 / ANCHOR) * decode(shares[s], BOUND_A)
                moment = momentum_rate * m_v[rows] + (a_v[rows] - mean)
                nm_v[rows] = jnp.where(alive[s], moment, 0.0)
    stores = []
    for j in range(lanes):
        stores.append(pltpu.make_async_copy(nm_v.at[j], nm_hbm.at[:, :, pl.ds(128 * j, 128)], store_sem.at[j]))
        stores[-1].start()

    for k in range(stripe):
        for i in range(1, n_rep):
            there = (x + i) % n_rep
            place = table.at[there, k]
            pltpu.make_async_copy(place, place, t_recv.at[k, there]).wait()
        pairs = table[:n_rep, k].reshape(n_rep * n_p, width)
        low = jnp.concatenate([pairs & 255, (pairs >> 16) & 255], axis=0)
        high = jnp.concatenate([(pairs >> 8) & 255, pairs >> 24], axis=0)
        picked = []
        for part in (low, high):
            part = part.astype(jnp.float32).astype(jnp.bfloat16)
            picked.append(jnp.dot(picker[...], part, preferred_element_type=jnp.float32))
        code = picked[0] + 256.0 * picked[1]
        code = jnp.where(code >= 32768.0, code - 65536.0, code)
        out_v[k] = decode(code, BOUND_N)
        stores.append(pltpu.make_async_copy(out_v.at[k], nw_hbm.at[k], store_sem.at[lanes + k]))
        stores[-1].start()

    for k in range(stripe):
        for i in range(n_rep):

            @pl.when(jnp.logical_not(diagonal & (x == i)))
            def _():
                f1_copy(k, i).wait_send()

            @pl.when(x != i)
            def _():
                pass_on(k, i).wait_send()

        for step in range(1, n_rep):
            r_copy(k, step).wait_send()
        settle(a_out, a_in, a_send, a_recv, k)
        settle(d_out, d_in, d_send, d_recv, k)
    for store in stores:
        store.wait()


def local(local_weights, anchor, momentum, owners):
    n_rep = lax.axis_size("rep")
    n_p = lax.axis_size("own") // n_rep
    blocks = owners.shape[0]
    stripe, width = local_weights.shape[2:]
    lanes = width // 128
    group = 2 * n_p
    rows = jnp.transpose(local_weights[0], (1, 0, 2))
    tall = (lanes, *anchor.shape[:2], 128)
    pairs = (stripe, n_p, width)
    vmem, dma = pltpu.VMEM, pltpu.SemaphoreType.DMA
    new_weights, new_momentum = pl.pallas_call(
        functools.partial(kernel, n_rep, n_p, stripe, width, blocks),
        out_shape=(
            jax.ShapeDtypeStruct(rows.shape, jnp.float32),
            jax.ShapeDtypeStruct(momentum.shape, jnp.float32),
        ),
        in_specs=[pl.BlockSpec(memory_space=pltpu.HBM)] * 4,
        out_specs=(pl.BlockSpec(memory_space=pl.ANY),) * 2,
        scratch_shapes=[
            vmem((1, blocks), jnp.int32),
            vmem(rows.shape, jnp.bfloat16),
            vmem(tall, jnp.float32),
            vmem(tall, jnp.float32),
            vmem(tall, jnp.float32),
            vmem((n_rep * group, blocks), jnp.bfloat16),
            vmem((blocks, n_rep * group), jnp.bfloat16),
            vmem((n_rep, stripe, group, width), jnp.bfloat16),
            vmem((n_rep, stripe, group, width), jnp.bfloat16),
            vmem(pairs, jnp.int32),
            vmem(pairs, jnp.int32),
            vmem(pairs, jnp.int32),
            vmem(pairs, jnp.int32),
            vmem((2 * n_rep, *pairs), jnp.int32),
            vmem(rows.shape, jnp.float32),
            dma((2 + 2 * lanes,)),
            dma((lanes + stripe,)),
            dma((stripe, n_rep)),
            dma((stripe, n_rep)),
            dma((stripe, n_p)),
            dma((stripe, n_p)),
            dma((stripe, n_p)),
            dma((stripe, n_p)),
            dma((stripe, n_rep - 1)),
            dma((stripe, n_rep)),
            dma((stripe, n_rep)),
            dma((stripe, n_rep)),
            pltpu.SemaphoreType.REGULAR((2,)),
            pltpu.SemaphoreType.REGULAR,
        ],
        compiler_params=pltpu.CompilerParams(collective_id=0, has_side_effects=True, vmem_limit_bytes=64000000),
    )(owners.reshape(1, blocks), rows, anchor, momentum)
    return jnp.transpose(new_weights, (1, 0, 2)), new_momentum


def solution(mesh):
    return jax.shard_map(
        local,
        mesh=mesh,
        in_specs=(P("rep", None, "own", None), P("own", "rep", None), P("own", "rep", None), P()),
        out_specs=(P(None, "own", None), P("own", "rep", None)),
        check_vma=False,
    )
```
